128 devices in a mesh: dom: 16 (over z, x), band: 8 (over y, core).
Axes of the slice: x: 4, y: 4, z: 4, core: 2. Of those that a mesh axis runs over, the one named last changes fastest.
Arguments:
- states: float32 [320, 96, 3584], P('band', 'dom'), may hold values from -6 to 6
- potential: float32 [96, 3584], P('dom'), may hold values from -4 to 1
- counts: int32 [8], replicated, may hold values from 1 to 40, 256 in all
Outputs:
- filtered: float32 [320, 96, 3584], P('band', 'dom')
- projected: float32 [2, 320, 320], P(None, 'band', 'dom')
The draws below stay inside these ranges and needn't reach their ends.
Inputs may be any that keep to these rules, and one draw needn't show every extreme that they name: The counts sum to 256; the largest equals 40.
All inputs are finite; a program needn't handle non-finite values.
Results may differ from the reference program's by a relative error of at most 0.000057.
Values sent between devices are 32-bit elements; how exact they have to be, the bound alone decides.
No kernel may reach another device: no remote copies, remote signals or barrier semaphores. Data moves between devices by JAX's collectives and lax.ppermute only.
A program may use at most 128 MiB of HBM per device.

```python
import math
import jax
import jax.numpy as jnp
import numpy as np
from jax import lax

BCAP = 40
STATES = 256
SLOTS = 320
NY = 56
NZ = 64
NX = 96
N_BAND = 8


def steps_of(rng, shape, shards, least, top_value):
    gain, own = 1.0, jax.random.fold_in(rng, 6)
    for axis_at, parts in shards:
        heights = jnp.exp(jax.random.uniform(jax.random.fold_in(own, axis_at), (parts,), jnp.float32, least / len(shards), top_value / len(shards)))
        gain = gain * jnp.repeat(heights, shape[axis_at] // parts).reshape([-1 if axis == axis_at else 1 for axis in range(len(shape))])
    return gain


def length_profile(number_of, total, most, slope):
    weights = [(1 << 20) // math.isqrt(standing ** slope) + 1 for standing in range(2, number_of + 1)]
    surplus, given = total - most - (number_of - 1), [1] * (number_of - 1)
    while surplus > 0:
        movable = [i for i in range(number_of - 1) if given[i] < most]
        whole, remaining = sum([weights[i] for i in movable]), surplus
        for i in movable:
            addition = min(most - given[i], max(1, remaining * weights[i] // whole), surplus)
            given[i] = given[i] + addition
            surplus = surplus - addition
    return np.array([most] + given)


def uneven_parts(own_key, number_of, total, limit, skew):
    if number_of == 2:
        one = jax.random.randint(own_key, (), max(1, total - limit), min(limit, total - 1) + 1)
        return jnp.stack([one, total - one])
    sizes = jnp.asarray(length_profile(number_of, total, limit, skew), jnp.int32)
    couples = (number_of - 1) // 2
    source_of, receiver = sizes[1:1 + 2 * couples:2], sizes[2:2 + 2 * couples:2]
    slack = jnp.minimum(source_of - 1, limit - receiver)
    shifted = jax.random.randint(jax.random.fold_in(own_key, 1), (couples,), 0, 1 << 20) % (slack + 1)
    sizes = sizes.at[1:1 + 2 * couples:2].set(source_of - shifted).at[2:2 + 2 * couples:2].set(receiver + shifted)
    return sizes[jax.random.permutation(jax.random.fold_in(own_key, 2), number_of)]


def scatter_about(stream_key, shape, width, reach, shards=(), held_as=jnp.bfloat16):
    level = steps_of(stream_key, shape, shards, -0.22, 0.18) if shards else 1.0
    entries = jax.random.normal(stream_key, shape, jnp.float32) * width * level
    return jnp.minimum(jnp.maximum(entries, -reach), reach).astype(held_as)


def setup_inputs(seed: int = 0) -> dict:
    keys = jax.random.split(jax.random.key(seed), 4)
    states = scatter_about(keys[0], (SLOTS, NX, NY * NZ), 1.0, 6.0, ((0, 8), (1, 16)), jnp.float32)
    potential = jnp.clip(-4.0 + 5.0 * jax.random.uniform(keys[1], (NX, NY * NZ), jnp.float32) ** steps_of(keys[1], (NX, NY * NZ), ((0, 16),), -0.2, 0.2), -4.0, 1.0)
    counts = uneven_parts(keys[2], N_BAND, STATES, BCAP, 2).astype(jnp.int32)
    return {"states": states, "potential": potential, "counts": counts}


def stencil_weights():
    fact = math.factorial
    sides = [2.0 * (-1.0) ** (k + 1) * fact(6) ** 2 / (k * k * fact(6 - k) * fact(6 + k)) for k in range(1, 7)]
    return -2.0 * sum(sides), sides


def apply_hamiltonian(field, potential):
    center_weight, side_weights = stencil_weights()
    span_x, span_y, span_z = field.shape[1], field.shape[2], field.shape[3]
    padded = jnp.pad(field, ((0, 0), (6, 6), (6, 6), (6, 6)))
    total = 3.0 * center_weight * field
    for step in range(1, 7):
        factor = side_weights[step - 1]
        near = padded[:, 6 + step:6 + step + span_x, 6:6 + span_y, 6:6 + span_z]
        near = near + padded[:, 6 - step:6 - step + span_x, 6:6 + span_y, 6:6 + span_z]
        near = near + padded[:, 6:6 + span_x, 6 + step:6 + step + span_y, 6:6 + span_z]
        near = near + padded[:, 6:6 + span_x, 6 - step:6 - step + span_y, 6:6 + span_z]
        near = near + padded[:, 6:6 + span_x, 6:6 + span_y, 6 + step:6 + step + span_z]
        near = near + padded[:, 6:6 + span_x, 6:6 + span_y, 6 - step:6 - step + span_z]
        total = total + factor * near
    return potential[None] * field - 0.5 * (1.0 / 0.36) * total


def reference(states, potential, counts):
    slot_ids = jnp.arange(BCAP, dtype=jnp.int32)
    keep = (slot_ids[None, :] < counts[:, None]).astype(jnp.float32).reshape(SLOTS)
    grid_states = states.reshape(SLOTS, NX, NY, NZ)
    grid_potential = potential.reshape(NX, NY, NZ)
    start = grid_states * keep[:, None, None, None]
    first = (apply_hamiltonian(start, grid_potential) - 11.0 * start) / 11.0
    second = 2.0 * (apply_hamiltonian(first, grid_potential) - 11.0 * first) / 11.0 - start
    filtered = 2.0 * (apply_hamiltonian(second, grid_potential) - 11.0 * second) / 11.0 - first
    image = apply_hamiltonian(filtered, grid_potential)
    flat_states = filtered.reshape(SLOTS, -1)
    flat_image = image.reshape(SLOTS, -1)
    intersection = jnp.dot(flat_states, flat_states.T, preferred_element_type=jnp.float32, precision=lax.Precision.HIGHEST)
    hamilton = jnp.dot(flat_image, flat_states.T, preferred_element_type=jnp.float32, precision=lax.Precision.HIGHEST)
    return filtered.reshape(SLOTS, NX, NY * NZ), jnp.stack([intersection, hamilton])
```

```python
import math

import jax
import jax.numpy as jnp
import ml_dtypes
import numpy as np
from jax import lax
from jax.experimental import pallas as pl
from jax.experimental.pallas import tpu as pltpu
from jax.sharding import PartitionSpec as P

NY = 56
NZ = 64
NX = 96
CELLS = NY * NZ
TILES = CELLS // 128
CAP = 40
PLANES = 6
EDGE = 384
WIDE = CELLS + 2 * EDGE
ROWS = PLANES * TILES
VMEM = 60 * 1024 * 1024
F32 = jnp.float32
BF16 = jnp.bfloat16


def stencil_weights():
    fact = math.factorial
    sides = [
        2.0 * (-1.0) ** (k + 1) * fact(6) ** 2 / (k * k * fact(6 - k) * fact(6 + k))
        for k in range(1, 7)
    ]
    return (-2.0 * sum(sides), sides)


CENTER, SIDES = stencil_weights()
KINETIC = -0.5 * (1.0 / 0.36)
STEP = [KINETIC * s for s in SIDES]


def halves(matrix):
    exact = matrix.astype(np.float32)
    high = exact.astype(ml_dtypes.bfloat16)
    low = (exact - high.astype(np.float32)).astype(ml_dtypes.bfloat16)
    return high, low


def band_matrix(size):
    out = np.zeros((size, size))
    for k in range(1, 7):
        for i in range(size - k):
            out[i, i + k] = out[i + k, i] = STEP[k - 1]
    return out


def stencil_operands():
    zh, zl = halves(np.kron(np.eye(4), band_matrix(NZ)))
    xh, xl = halves(band_matrix(NX))
    return np.concatenate([zh, zh, zl], axis=0), np.concatenate([xh, xh, xl], axis=1)


def cost(flops, nbytes):
    return pl.CostEstimate(flops=flops, transcendentals=0, bytes_accessed=nbytes)


def params():
    return pltpu.CompilerParams(vmem_limit_bytes=VMEM)


SMEM_SPEC = pl.BlockSpec(memory_space=pltpu.SMEM)


def pack_body(info, states, pot, out0, out1, out2, flat):
    live = info[0]
    lanes = lax.broadcasted_iota(jnp.int32, (8, 128), 0)
    for r in range(TILES):
        flat[pl.ds(r, PLANES, stride=TILES), :] = pot[:, r * 128 : (r + 1) * 128]
    for p in range(PLANES):
        piece = flat[p * TILES : (p + 1) * TILES, :]
        for d in range(16):
            base = (d * PLANES + p) * 2 * TILES + TILES
            out0[base : base + TILES, :] = piece

    def plane(p, carry):
        for i in range(5):
            keep = (lanes + 8 * i) < live
            for r in range(TILES):
                v = states[p, 8 * i : 8 * i + 8, r * 128 : (r + 1) * 128]
                v = jnp.where(keep, v, 0.0)
                if i < 2:
                    out0[pl.ds(8 * i * 2 * ROWS + p * 2 * TILES + r, 8, stride=2 * ROWS), :] = v
                elif i < 4:
                    out1[pl.ds(8 * (i - 2) * ROWS + p * TILES + r, 8, stride=ROWS), :] = v
                else:
                    for q in range(2):
                        out2[pl.ds(8 * q * ROWS + p * TILES + r, 8, stride=ROWS), :] = v
        return carry

    lax.fori_loop(0, PLANES, plane, 0)


def pack(info, states, pot):
    return pl.pallas_call(
        pack_body,
        out_shape=(
            jax.ShapeDtypeStruct((16 * 2 * ROWS, 128), F32),
            jax.ShapeDtypeStruct((16 * ROWS, 128), F32),
            jax.ShapeDtypeStruct((16 * ROWS, 128), F32),
        ),
        in_specs=[SMEM_SPEC, pl.BlockSpec(), pl.BlockSpec()],
        scratch_shapes=[pltpu.VMEM((ROWS, 128), F32)],
        compiler_params=params(),
        cost_estimate=cost(4_000_000, 10_000_000),
        name="pack",
    )(info, states, pot)


def split(value):
    high = value.astype(BF16)
    return high, (value - high.astype(F32)).astype(BF16)


def comp_body(first, half, *refs):
    if first:
        recv, wz, ax, out, diag = refs[:5]
        refs = refs[5:]
    elif half:
        info, recv, diag, wz, ax, out = refs[:6]
        refs = refs[6:]
    else:
        recv, diag, wz, ax, out = refs[:5]
        refs = refs[5:]
    va, vb, ua, ub, ha, hb, la, lb = refs
    stride = 2 * TILES if first else TILES
    zero = jnp.zeros((NX, EDGE), F32)
    for ref in (va, vb, ua, ub):
        ref[:, :EDGE] = zero
        ref[:, EDGE + CELLS :] = zero

    def load(r, carry):
        at = pl.multiple_of(r * 128, 128)
        tiles = [recv[pl.ds(8 * i * stride + r, 8, stride=stride), :] for i in range(12)]
        v = jnp.concatenate(tiles, axis=0)
        va[:, pl.ds(EDGE + at, 128)] = v
        ua[:, pl.ds(EDGE + at, 128)] = pltpu.roll(v, 64, 1)
        high, low = split(v)
        ha[:, pl.ds(at, 128)] = high
        la[:, pl.ds(at, 128)] = low
        if first:
            tiles = [
                recv[pl.ds(8 * i * stride + TILES + r, 8, stride=stride), :] for i in range(12)
            ]
            diag[:, pl.ds(at, 128)] = jnp.concatenate(tiles, axis=0) + KINETIC * 3.0 * CENTER
        return carry

    lax.fori_loop(0, TILES, load, 0)
    low_half = (lax.broadcasted_iota(jnp.int32, (NX, 256), 1) % 128) < 64

    def apply(src, dst, stage):
        v_src, u_src, h_src, l_src = src
        v_dst, u_dst, h_dst, l_dst = dst

        def block(cb, carry):
            at = pl.multiple_of(cb * 256, 256)

            def v_at(k):
                return v_src[:, pl.ds(EDGE + at + 128 * k, 256)]

            def u_at(k):
                return u_src[:, pl.ds(EDGE + at + 128 * k, 384)]

            h = h_src[:, pl.ds(at, 256)]
            l = l_src[:, pl.ds(at, 256)]
            acc = jnp.dot(
                jnp.concatenate([h, l, h], axis=1), wz[...], preferred_element_type=F32
            )
            acc = acc + jnp.dot(
                ax[...], jnp.concatenate([h, l, h], axis=0), preferred_element_type=F32
            )
            odd = STEP[0] * (u_at(0) + u_at(-1))
            odd = odd + STEP[2] * (u_at(1) + u_at(-2))
            odd = odd + STEP[4] * (u_at(2) + u_at(-3))
            acc = acc + jnp.where(low_half, odd[:, :256], odd[:, 128:])
            acc = acc + STEP[1] * (v_at(1) + v_at(-1))
            acc = acc + STEP[3] * (v_at(2) + v_at(-2))
            acc = acc + STEP[5] * (v_at(3) + v_at(-3))
            v = v_at(0)
            new = acc + diag[:, pl.ds(at, 256)] * v
            if stage == 1:
                new = new * (1.0 / 11.0) - v
            elif stage < 4:
                new = new * (2.0 / 11.0) - 2.0 * v - v_dst[:, pl.ds(EDGE + at, 256)]
            v_dst[:, pl.ds(EDGE + at, 256)] = new
            if stage < 4:
                for j in range(2):
                    u_dst[:, pl.ds(EDGE + at + 128 * j, 128)] = pltpu.roll(
                        new[:, 128 * j : 128 * j + 128], 64, 1
                    )
                high, low = split(new)
                h_dst[:, pl.ds(at, 256)] = high
                l_dst[:, pl.ds(at, 256)] = low
            return carry

        lax.fori_loop(0, CELLS // 256, block, 0)

    a, b = (va, ua, ha, la), (vb, ub, hb, lb)
    apply(a, b, 1)
    apply(b, a, 2)
    apply(a, b, 3)
    apply(b, a, 4)
    count = TILES // 2 if half else TILES
    begin = info[1] * (count * 128) if half else 0

    def store(r, carry):
        at = pl.multiple_of(EDGE + begin + r * 128, 128)
        for which, ref in ((0, vb), (1, va)):
            for i in range(12):
                out[pl.ds(8 * i * 2 * count + which * count + r, 8, stride=2 * count), :] = ref[
                    8 * i : 8 * i + 8, pl.ds(at, 128)
                ]
        return carry

    lax.fori_loop(0, count, store, 0)


def comp(first, half, args, name):
    rows = NX * TILES * (1 if half else 2)
    out_shape = [jax.ShapeDtypeStruct((rows, 128), F32)]
    if first:
        out_shape.append(jax.ShapeDtypeStruct((NX, CELLS), F32))
    wide = pltpu.VMEM((NX, WIDE), F32)
    narrow = pltpu.VMEM((NX, CELLS), BF16)
    in_specs = [pl.BlockSpec()] * len(args)
    if half:
        in_specs[0] = SMEM_SPEC

    def body(*refs):
        comp_body(first, half, *refs)

    return pl.pallas_call(
        body,
        out_shape=tuple(out_shape),
        in_specs=in_specs,
        scratch_shapes=[wide] * 4 + [narrow] * 4,
        compiler_params=params(),
        cost_estimate=cost(15_000_000_000, 10_000_000),
        name=name,
    )(*args)


def unpack_body(recv0, recv1, recv2, filtered, send_f, send_i):
    for p in range(PLANES):
        for r in range(TILES):
            b, t = divmod(p * TILES + r, 21)
            for which in range(2):
                send = send_i if which else send_f
                for i in range(5):
                    if i < 4:
                        recv = recv0 if i < 2 else recv1
                        start = 8 * (i % 2) * 2 * ROWS + p * 2 * TILES + which * TILES + r
                        v = recv[pl.ds(start, 8, stride=2 * ROWS), :]
                    else:
                        q, rest = divmod(r, TILES // 2)
                        start = 8 * q * ROWS + p * TILES + which * (TILES // 2) + rest
                        v = recv2[pl.ds(start, 8, stride=ROWS), :]
                    rows = slice(8 * i, 8 * i + 8)
                    send[b, rows, t * 128 : (t + 1) * 128] = v
                    if not which:
                        filtered[p, rows, r * 128 : (r + 1) * 128] = v


def unpack(recv0, recv1, recv2):
    return pl.pallas_call(
        unpack_body,
        out_shape=(
            jax.ShapeDtypeStruct((PLANES, CAP, CELLS), F32),
            jax.ShapeDtypeStruct((8, CAP, 21 * 128), F32),
            jax.ShapeDtypeStruct((8, CAP, 21 * 128), F32),
        ),
        compiler_params=params(),
        cost_estimate=cost(4_000_000, 17_000_000),
        name="unpack",
    )(recv0, recv1, recv2)


KSTEP = 7 * 128


def product(left, right):
    lh, ll = split(left)
    rh, rl = split(right)
    total = None
    for one, two in ((lh, rh), (lh, rl), (ll, rh)):
        term = lax.dot_general(one, two, (((1,), (1,)), ((), ())), preferred_element_type=F32)
        total = term if total is None else total + term
    return total


def overlap_body(left, out):
    term = product(left[...], left[...])

    @pl.when(pl.program_id(0) == 0)
    def _():
        out[...] = term

    @pl.when(pl.program_id(0) > 0)
    def _():
        out[...] += term


def overlap(full):
    n = full.shape[0]
    return pl.pallas_call(
        overlap_body,
        grid=(3,),
        out_shape=jax.ShapeDtypeStruct((n, n), F32),
        in_specs=[pl.BlockSpec((n, KSTEP), lambda k: (0, k))],
        out_specs=pl.BlockSpec((n, n), lambda k: (0, 0)),
        compiler_params=params(),
        cost_estimate=cost(2_000_000_000, 4_000_000),
        name="overlap",
    )(full)


def energy_body(left, right, inter, out, acc):
    term = product(left[...], right[...])

    @pl.when(pl.program_id(0) == 0)
    def _():
        acc[...] = term

    @pl.when(pl.program_id(0) > 0)
    def _():
        acc[...] += term

    @pl.when(pl.program_id(0) == 2)
    def _():
        for d in range(16):
            out[d, :20, :] = inter[20 * d : 20 * d + 20, :]
            out[d, 20:40, :] = acc[20 * d : 20 * d + 20, :]


def energy(full, image, inter):
    n = full.shape[0]
    return pl.pallas_call(
        energy_body,
        grid=(3,),
        out_shape=jax.ShapeDtypeStruct((16, 40, n), F32),
        in_specs=[
            pl.BlockSpec((n, KSTEP), lambda k: (0, k)),
            pl.BlockSpec((n, KSTEP), lambda k: (0, k)),
            pl.BlockSpec((n, n), lambda k: (0, 0)),
        ],
        out_specs=pl.BlockSpec((16, 40, n), lambda k: (0, 0, 0)),
        scratch_shapes=[pltpu.VMEM((n, n), F32)],
        compiler_params=params(),
        cost_estimate=cost(2_000_000_000, 8_000_000),
        name="energy",
    )(full, image, inter)


def exchange(value, axis, parts):
    shape = value.shape
    value = value.reshape((parts, -1) + shape[-1:])
    return lax.all_to_all(value, axis, 0, 0, tiled=True).reshape(shape)


def local(states, potential, counts):
    wz, ax = (jnp.asarray(m) for m in stencil_operands())
    live = counts[lax.axis_index("band")]
    info = jnp.stack([live, lax.axis_index("dom") // 8]).astype(jnp.int32)
    send0, send1, send2 = pack(info, jnp.transpose(states, (1, 0, 2)), potential)
    recv0 = exchange(send0, "dom", 16)
    recv0, send1 = lax.optimization_barrier((recv0, send1))
    recv1 = exchange(send1, "dom", 16)
    out0, diag = comp(True, False, (recv0, wz, ax), "comp0")
    recv1, send2 = lax.optimization_barrier((recv1, send2))
    recv2 = exchange(send2, "dom", 16)
    (out1,) = comp(False, False, (recv1, diag, wz, ax), "comp1")
    recv2, out0 = lax.optimization_barrier((recv2, out0))
    back0 = exchange(out0, "dom", 16)
    (out2,) = comp(False, True, (info, recv2, diag, wz, ax), "comp2")
    back0, out1 = lax.optimization_barrier((back0, out1))
    back1 = exchange(out1, "dom", 16)
    back1, out2 = lax.optimization_barrier((back1, out2))
    back2 = exchange(out2, "dom", 16)
    filtered, send_f, send_i = unpack(back0, back1, back2)
    full = lax.all_to_all(send_f, "band", 0, 0, tiled=True)
    full, send_i = lax.optimization_barrier((full, send_i))
    image = lax.all_to_all(send_i, "band", 0, 0, tiled=True)
    full = full.reshape(8 * CAP, 21 * 128)
    image = image.reshape(8 * CAP, 21 * 128)
    terms = energy(full, image, overlap(full))
    terms = lax.all_to_all(terms, "dom", 0, 0, tiled=True).sum(axis=0)
    terms = jnp.transpose(terms.reshape(2, 20, 8, CAP), (2, 0, 1, 3)).reshape(8, 40, CAP)
    terms = lax.all_to_all(terms, "band", 0, 0, tiled=True).sum(axis=0)
    projected = jnp.transpose(terms.reshape(2, 20, CAP), (0, 2, 1))
    return (jnp.transpose(filtered, (1, 0, 2)), projected)


def solution(mesh):
    return jax.shard_map(
        local,
        mesh=mesh,
        in_specs=(P("band", "dom", None), P("dom", None), P()),
        out_specs=(P("band", "dom", None), P(None, "band", "dom")),
        check_vma=False,
    )
```

```python
import math

import jax
import jax.numpy as jnp
import ml_dtypes
import numpy as np
from jax import lax
from jax.experimental import pallas as pl
from jax.experimental.pallas import tpu as pltpu
from jax.sharding import PartitionSpec as P

NY = 56
NZ = 64
NX = 96
CELLS = NY * NZ
TILES = CELLS // 128
CAP = 40
PLANES = 6
EDGE = 384
WIDE = CELLS + 2 * EDGE
ROWS = PLANES * TILES
HALF = 16
QUAD = 4
GROUP = 512
LINE = TILES + QUAD
PARTS = 21
MAIN = 32
SHARE = 11
VMEM = 60 * 1024 * 1024
F32 = jnp.float32
BF16 = jnp.bfloat16


def stencil_weights():
    fact = math.factorial
    sides = [
        2.0 * (-1.0) ** (k + 1) * fact(6) ** 2 / (k * k * fact(6 - k) * fact(6 + k))
        for k in range(1, 7)
    ]
    return (-2.0 * sum(sides), sides)


CENTER, SIDES = stencil_weights()
KINETIC = -0.5 * (1.0 / 0.36)
SCALE = 2.0 / 11.0
STEP = [SCALE * KINETIC * s for s in SIDES]


def halves(matrix):
    exact = matrix.astype(np.float32)
    high = exact.astype(ml_dtypes.bfloat16)
    low = (exact - high.astype(np.float32)).astype(ml_dtypes.bfloat16)
    return high, low


def band_matrix(size):
    out = np.zeros((size, size))
    for k in range(1, 7):
        for i in range(size - k):
            out[i, i + k] = out[i + k, i] = STEP[k - 1]
    return out


def stencil_operands():
    zh, zl = halves(np.kron(np.eye(4), band_matrix(NZ)))
    xh, xl = halves(band_matrix(NX))
    return np.concatenate([zh, zh, zl], axis=0), np.concatenate([xh, xh, xl], axis=1)


def cost(flops, nbytes):
    return pl.CostEstimate(flops=flops, transcendentals=0, bytes_accessed=nbytes)


def params():
    return pltpu.CompilerParams(vmem_limit_bytes=VMEM)


SMEM_SPEC = pl.BlockSpec(memory_space=pltpu.SMEM)


def pack_body(info, states, pot, out0, out1, out2):
    live = info[0]
    lanes = lax.broadcasted_iota(jnp.int32, (8, 128), 0)
    first = pl.multiple_of(jnp.minimum(info[2], 6) * (QUAD * 128), 128)
    for p in range(PLANES):
        tiles = [pot[p : p + 1, pl.ds(first + e * 128, 128)] for e in range(QUAD)]
        piece = jnp.concatenate(tiles, axis=0)
        for d in range(16):
            base = (d * PLANES + p) * LINE + TILES
            out0[base : base + QUAD, :] = piece

    def plane(p, carry):
        for i in range(5):
            keep = (lanes + 8 * i) < live
            for r in range(TILES):
                v = states[p, 8 * i : 8 * i + 8, r * 128 : (r + 1) * 128]
                v = jnp.where(keep, v, 0.0)
                if i < 2:
                    out0[pl.ds(8 * i * PLANES * LINE + p * LINE + r, 8, stride=PLANES * LINE), :] = v
                elif i < 4:
                    out1[pl.ds(8 * (i - 2) * ROWS + p * TILES + r, 8, stride=ROWS), :] = v
                else:
                    for q in range(2):
                        out2[pl.ds(8 * q * ROWS + p * TILES + r, 8, stride=ROWS), :] = v
        return carry

    lax.fori_loop(0, PLANES, plane, 0)


def pack(info, states, pot):
    return pl.pallas_call(
        pack_body,
        out_shape=(
            jax.ShapeDtypeStruct((NX * LINE, 128), F32),
            jax.ShapeDtypeStruct((16 * ROWS, 128), F32),
            jax.ShapeDtypeStruct((16 * ROWS, 128), F32),
        ),
        in_specs=[SMEM_SPEC, pl.BlockSpec(), pl.BlockSpec()],
        compiler_params=params(),
        cost_estimate=cost(4_000_000, 10_000_000),
        name="pack",
    )(info, states, pot)


def split(value):
    high = value.astype(BF16)
    return high, (value - high.astype(F32)).astype(BF16)


def comp_body(first, half, *refs):
    if first:
        info, recv = refs[:2]
        pots = refs[2:10]
        wz, ax, out, image, diag = refs[10:15]
        refs = refs[15:]
    elif half:
        info, recv, diag, wz, ax, out, image, part = refs[:8]
        refs = refs[8:]
    else:
        recv, diag, wz, ax, out, image = refs[:6]
        refs = refs[6:]
    va, vb, ua, ub, ha, hb, la, lb, az, ay = refs
    stride = LINE if first else TILES
    zero = jnp.zeros((NX, EDGE), F32)
    for ref in (va, vb, ua, ub):
        ref[:, :EDGE] = zero
        ref[:, EDGE + CELLS :] = zero

    def load(r, carry):
        at = pl.multiple_of(r * 128, 128)
        tiles = [recv[pl.ds(8 * i * stride + r, 8, stride=stride), :] for i in range(12)]
        v = jnp.concatenate(tiles, axis=0)
        va[:, pl.ds(EDGE + at, 128)] = v
        ua[:, pl.ds(EDGE + at, 128)] = pltpu.roll(v, 64, 1)
        high, low = split(v)
        ha[:, pl.ds(at, 128)] = high
        la[:, pl.ds(at, 128)] = low
        return carry

    lax.fori_loop(0, TILES, load, 0)
    if first:
        for s in range(8):
            whose = info[2] ^ s

            @pl.when(whose < 7)
            def _():
                for e in range(QUAD):
                    at = pl.multiple_of(whose * (QUAD * 128) + e * 128, 128)
                    tiles = [
                        pots[s][pl.ds(8 * i * QUAD + e, 8, stride=QUAD), :] for i in range(12)
                    ]
                    diag[:, pl.ds(at, 128)] = (
                        SCALE * (jnp.concatenate(tiles, axis=0) + KINETIC * 3.0 * CENTER) - 2.0
                    )

    low_half = (lax.broadcasted_iota(jnp.int32, (8, GROUP), 1) % 128) < 64

    def apply(src, dst, stage):
        v_src, u_src, h_src, l_src = src
        v_dst, u_dst, h_dst, l_dst = dst

        def products(at):
            lefts = []
            for j in range(GROUP // 256):
                h = h_src[:, pl.ds(at + 256 * j, 256)]
                l = l_src[:, pl.ds(at + 256 * j, 256)]
                lefts.append(jnp.concatenate([h, l, h], axis=1))
            along_z = jnp.dot(
                jnp.concatenate(lefts, axis=0), wz[...], preferred_element_type=F32
            )
            h = h_src[:, pl.ds(at, GROUP)]
            l = l_src[:, pl.ds(at, GROUP)]
            along_x = jnp.dot(
                ax[...], jnp.concatenate([h, l, h], axis=0), preferred_element_type=F32
            )
            return along_z, along_x

        az[...], ay[...] = products(0)

        def block(group, carry):
            at = pl.multiple_of(group * GROUP, GROUP)
            after = jnp.minimum(group + 1, CELLS // GROUP - 1)
            next_z, next_x = products(pl.multiple_of(after * GROUP, GROUP))
            pending = []
            for i in range(12):
                rows = slice(8 * i, 8 * i + 8)
                v = v_src[rows, pl.ds(at, GROUP + 2 * EDGE)]
                u = u_src[rows, pl.ds(at, GROUP + 2 * EDGE)]

                def v_at(k):
                    return v[:, EDGE + 128 * k : EDGE + 128 * k + GROUP]

                def u_at(k):
                    return u[:, EDGE + 128 * k : EDGE + 128 * k + GROUP + 128]

                odd = STEP[0] * (u_at(0) + u_at(-1))
                odd = odd + STEP[2] * (u_at(1) + u_at(-2))
                odd = odd + STEP[4] * (u_at(2) + u_at(-3))
                even = STEP[1] * (v_at(1) + v_at(-1))
                even = even + STEP[3] * (v_at(2) + v_at(-2))
                even = even + STEP[5] * (v_at(3) + v_at(-3))
                near = even + jnp.where(low_half, odd[:, :GROUP], odd[:, 128:])
                center = v_at(0)
                new = near + diag[rows, pl.ds(at, GROUP)] * center
                new = new + ay[rows, :]
                across = [slice(NX * j + 8 * i, NX * j + 8 * i + 8) for j in range(GROUP // 256)]
                new = new + jnp.concatenate([az[strip, :] for strip in across], axis=1)
                ay[rows, :] = next_x[rows, :]
                for strip in across:
                    az[strip, :] = next_z[strip, :]
                if stage == 1:
                    new = 0.5 * new
                elif stage < 4:
                    new = new - v_dst[rows, pl.ds(EDGE + at, GROUP)]
                else:
                    new = 5.5 * new + 11.0 * center
                v_dst[rows, pl.ds(EDGE + at, GROUP)] = new
                if stage < 4:
                    for j in range(GROUP // 128):
                        u_dst[rows, pl.ds(EDGE + at + 128 * j, 128)] = pltpu.roll(
                            new[:, 128 * j : 128 * j + 128], 64, 1
                        )
                    pending.append(new)
                    if i % 2:
                        high, low = split(jnp.concatenate(pending, axis=0))
                        pair = slice(8 * i - 8, 8 * i + 8)
                        h_dst[pair, pl.ds(at, GROUP)] = high
                        l_dst[pair, pl.ds(at, GROUP)] = low
                        pending = []
            return carry

        lax.fori_loop(0, CELLS // GROUP, block, 0)

    a, b = (va, ua, ha, la), (vb, ub, hb, lb)
    apply(a, b, 1)
    apply(b, a, 2)
    apply(a, b, 3)
    apply(b, a, 4)
    outs = [(out, 1, 0), (image, 0, 0)]
    if half:
        outs.append((part, 1, info[1] * (12 * 128)))

    for ref, which, begin in outs:
        count = ref.shape[0] // NX

        def store(r, carry):
            at = pl.multiple_of(EDGE + begin + r * 128, 128)
            for i in range(12):
                ref[pl.ds(8 * i * count + r, 8, stride=count), :] = (vb if which else va)[
                    8 * i : 8 * i + 8, pl.ds(at, 128)
                ]
            return carry

        lax.fori_loop(0, count, store, 0)


def comp(first, half, args):
    out_shape = [jax.ShapeDtypeStruct((NX * TILES, 128), F32)] * 2
    if first:
        out_shape.append(jax.ShapeDtypeStruct((NX, CELLS), F32))
    if half:
        out_shape.append(jax.ShapeDtypeStruct((NX * HALF, 128), F32))
    wide = pltpu.VMEM((NX, WIDE), F32)
    narrow = pltpu.VMEM((NX, CELLS), BF16)
    in_specs = [pl.BlockSpec()] * len(args)
    if first or half:
        in_specs[0] = SMEM_SPEC

    def body(*refs):
        comp_body(first, half, *refs)

    return pl.pallas_call(
        body,
        out_shape=tuple(out_shape),
        in_specs=in_specs,
        scratch_shapes=[wide] * 4
        + [narrow] * 4
        + [pltpu.VMEM((NX * GROUP // 256, 256), F32), pltpu.VMEM((NX, GROUP), F32)],
        compiler_params=params(),
        cost_estimate=cost(15_000_000_000, 10_000_000),
    )(*args)


def unpack_main_body(later, *refs):
    info, recv = refs[:2]
    filtered, *sends = refs[3:12] if later else refs[2:11]
    send = refs[-1]
    for p in range(PLANES):
        for r in range(TILES):
            b, t = divmod(p * TILES + r, PARTS)
            for i in range(2):
                v = recv[pl.ds(8 * i * ROWS + p * TILES + r, 8, stride=ROWS), :]
                rows = slice(8 * i, 8 * i + 8)
                send[b ^ info[2], rows, t * 128 : (t + 1) * 128] = v
                filtered[p, rows, r * 128 : (r + 1) * 128] = v
    for s in range(8):
        sends[s][...] = send[s]


def unpack_main(info, recv, base):
    later = base is not None
    which = int(later)

    def body(*refs):
        unpack_main_body(later, *refs)

    in_specs = [SMEM_SPEC, pl.BlockSpec((16 * ROWS, 128), lambda i: (0, 0))]
    args = (info, recv)
    if later:
        in_specs.append(pl.BlockSpec(memory_space=pl.ANY))
        args += (base,)
    return pl.pallas_call(
        body,
        grid=(1,),
        out_shape=(jax.ShapeDtypeStruct((PLANES, CAP, CELLS), F32),)
        + (jax.ShapeDtypeStruct((16, PARTS * 128), F32),) * 8,
        in_specs=in_specs,
        out_specs=(pl.BlockSpec((PLANES, 16, CELLS), lambda i: (0, which, 0)),)
        + (pl.BlockSpec((16, PARTS * 128), lambda i: (0, 0)),) * 8,
        scratch_shapes=[pltpu.VMEM((8, 16, PARTS * 128), F32)],
        input_output_aliases={2: 0} if later else {},
        compiler_params=params(),
        cost_estimate=cost(4_000_000, 4_000_000),
    )(*args)


def unpack_rest_body(recv, base, filtered):
    for p in range(PLANES):
        for r in range(TILES):
            q = r // HALF
            start = 8 * q * PLANES * HALF + p * HALF + r - 12 * q
            filtered[p, :, r * 128 : (r + 1) * 128] = recv[
                pl.ds(start, 8, stride=PLANES * HALF), :
            ]


def unpack_rest(recv, base):
    return pl.pallas_call(
        unpack_rest_body,
        grid=(1,),
        out_shape=jax.ShapeDtypeStruct((PLANES, CAP, CELLS), F32),
        in_specs=[
            pl.BlockSpec((16 * PLANES * HALF, 128), lambda i: (0, 0)),
            pl.BlockSpec(memory_space=pl.ANY),
        ],
        out_specs=pl.BlockSpec((PLANES, 8, CELLS), lambda i: (0, 4, 0)),
        input_output_aliases={1: 0},
        compiler_params=params(),
        cost_estimate=cost(1_000_000, 2_000_000),
        name="unpack_rest",
    )(recv, base)


def share_body(info, img0, img1, img2, f2, out):
    second = info[1] > 0

    def group(big, carry):
        base = pl.multiple_of(big * 8 * PARTS, 8)
        to = pl.multiple_of(big * 8 * 64, 8)
        for g in range(8):
            at = base + PARTS * g
            row = to + 64 * g
            out[pl.ds(row, PARTS), :] = img0[pl.ds(at, PARTS), :]
            out[pl.ds(row + PARTS, PARTS), :] = img1[pl.ds(at, PARTS), :]
            for ref, start in ((img2, 2 * PARTS), (f2, 2 * PARTS + SHARE)):
                out[pl.ds(row + start, SHARE), :] = jnp.where(
                    second, ref[pl.ds(at + 10, SHARE), :], ref[pl.ds(at, SHARE), :]
                )
        return carry

    lax.fori_loop(0, 16, group, 0)


def share(info, img0, img1, img2, f2):
    return pl.pallas_call(
        share_body,
        out_shape=jax.ShapeDtypeStruct((128 * 64, 128), F32),
        in_specs=[SMEM_SPEC] + [pl.BlockSpec()] * 4,
        compiler_params=params(),
        cost_estimate=cost(2_000_000, 10_000_000),
        name="share",
    )(info, img0, img1, img2, f2)


SLOTS = 8 * CAP
SECOND = 384
BOTH = SECOND + SLOTS
KSTEP = 7 * 128


def gram_body(info, *refs):
    pieces, (rest, out, main, high, low, total) = refs[:16], refs[16:]
    for s in range(8):
        for k in range(2):
            main[info[2] ^ s, 16 * k : 16 * k + 16] = pieces[8 * k + s][...]
    high[SLOTS:SECOND, :] = jnp.zeros((SECOND - SLOTS, PARTS * 128), BF16)
    low[SLOTS:SECOND, :] = jnp.zeros((SECOND - SLOTS, PARTS * 128), BF16)

    def fill(t, carry, late):
        at = pl.multiple_of(t * 128, 128)
        f_rows = []
        i_rows = []
        for b in range(8):
            shared = [
                rest[
                    pl.ds((8 * late * 8 + b) * 64 + start + t - 10 * late, 8, stride=8 * 64), :
                ]
                for start in (2 * PARTS, 2 * PARTS + SHARE)
            ]
            f_rows += [main[b, :, pl.ds(at, 128)], shared[1]]
            for k in range(2):
                for half in range(2):
                    start = (64 * half + b) * 64 + PARTS * k + t
                    i_rows.append(rest[pl.ds(start, 8, stride=8 * 64), :])
            i_rows.append(shared[0])
        for rows, base in ((f_rows, 0), (i_rows, SECOND)):
            h, l = split(jnp.concatenate(rows, axis=0))
            high[base : base + SLOTS, pl.ds(at, 128)] = h
            low[base : base + SLOTS, pl.ds(at, 128)] = l
        return carry

    lax.fori_loop(0, SHARE, lambda t, c: fill(t, c, 0), 0)
    lax.fori_loop(SHARE, PARTS, lambda t, c: fill(t, c, 1), 0)
    for step in range(3):
        cols = slice(step * KSTEP, (step + 1) * KSTEP)
        term = None
        for one, two in ((high, high), (high, low), (low, high)):
            part = lax.dot_general(
                one[:SLOTS, cols],
                two[:, cols],
                (((1,), (1,)), ((), ())),
                preferred_element_type=F32,
            )
            term = part if term is None else term + part
        total[...] = term if step == 0 else total[...] + term
    for d in range(16):
        out[d, :20, :] = total[20 * d : 20 * d + 20, :SLOTS]
        out[d, 20:40, :] = total[20 * d : 20 * d + 20, SECOND:]


def gram(info, pieces, rest):
    return pl.pallas_call(
        gram_body,
        out_shape=jax.ShapeDtypeStruct((16, 40, SLOTS), F32),
        in_specs=[SMEM_SPEC] + [pl.BlockSpec()] * 17,
        scratch_shapes=[pltpu.VMEM((8, MAIN, PARTS * 128), F32)]
        + [pltpu.VMEM((BOTH, PARTS * 128), BF16)] * 2
        + [pltpu.VMEM((SLOTS, BOTH), F32)],
        compiler_params=params(),
        cost_estimate=cost(4_000_000_000, 8_000_000),
        name="gram",
    )(info, *pieces, rest)


def exchange(value, axis, parts):
    shape = value.shape
    value = value.reshape((parts, -1) + shape[-1:])
    return lax.all_to_all(value, axis, 0, 0, tiled=True).reshape(shape)


def swaps(pieces):
    out = [pieces[0]]
    for s in range(1, 8):
        pairs = [(b, b ^ s) for b in range(8)]
        out.append(lax.ppermute(pieces[s], "band", pairs))
    return out


def work(states, potential, counts):
    wz, ax = (jnp.asarray(m) for m in stencil_operands())
    band = lax.axis_index("band")
    info = jnp.stack([counts[band], lax.axis_index("dom") // 8, band]).astype(jnp.int32)
    send0, send1, send2 = pack(info, jnp.transpose(states, (1, 0, 2)), potential)
    recv0 = exchange(send0, "dom", 16)
    own = recv0.reshape(NX, LINE, 128)[:, TILES:, :].reshape(NX * QUAD, 128)
    pots = swaps([own] * 8)
    recv0, send1 = lax.optimization_barrier((recv0, send1))
    recv1 = exchange(send1, "dom", 16)
    out0, img0, diag = comp(True, False, (info, recv0, *pots, wz, ax))
    recv1, send2 = lax.optimization_barrier((recv1, send2))
    recv2 = exchange(send2, "dom", 16)
    out1, img1 = comp(False, False, (recv1, diag, wz, ax))
    recv2, out0 = lax.optimization_barrier((recv2, out0))
    back0 = exchange(out0, "dom", 16)
    filtered, *early = unpack_main(info, back0, None)
    early = swaps(early)
    recv2, filtered = lax.optimization_barrier((recv2, filtered))
    out2, img2, half2 = comp(False, True, (info, recv2, diag, wz, ax))
    back0, out1 = lax.optimization_barrier((back0, out1))
    back1 = exchange(out1, "dom", 16)
    back1, half2 = lax.optimization_barrier((back1, half2))
    back2 = exchange(half2, "dom", 16)
    filtered, *late = unpack_main(info, back1, filtered)
    late = swaps(late)
    img0, filtered = lax.optimization_barrier((img0, filtered))
    shared = share(info, img0, img1, img2, out2)
    back2, shared = lax.optimization_barrier((back2, shared))
    filtered = unpack_rest(back2, filtered)
    rest = exchange(shared, ("dom", "band"), 128)
    terms = gram(info, early + late, rest)
    terms = lax.all_to_all(terms, "dom", 0, 0, tiled=True).sum(axis=0)
    terms = jnp.transpose(terms.reshape(2, 20, 8, CAP), (2, 0, 1, 3)).reshape(8, 40, CAP)
    terms = lax.all_to_all(terms, "band", 0, 0, tiled=True).sum(axis=0)
    projected = jnp.transpose(terms.reshape(2, 20, CAP), (0, 2, 1))
    return (jnp.transpose(filtered, (1, 0, 2)), projected)


def solution(mesh):
    return jax.shard_map(
        work,
        mesh=mesh,
        in_specs=(P("band", "dom", None), P("dom", None), P()),
        out_specs=(P("band", "dom", None), P(None, "band", "dom")),
        check_vma=False,
    )
```

```python
import math

import jax
import jax.numpy as jnp
import ml_dtypes
import numpy as np
from jax import lax
from jax.experimental import pallas as pl
from jax.experimental.pallas import tpu as pltpu
from jax.sharding import PartitionSpec as P

NY = 56
NZ = 64
NX = 96
CELLS = NY * NZ
TILES = CELLS // 128
CAP = 40
PLANES = 6
EDGE = 384
WIDE = CELLS + 2 * EDGE
ROWS = PLANES * TILES
HALF = 16
QUAD = 4
GROUP = 512
LINE = TILES + QUAD
PARTS = 21
SHARE = 11
MAIN = 32
WIDTH = PARTS * 128
VMEM = 60 * 1024 * 1024
F32 = jnp.float32
BF16 = jnp.bfloat16


def stencil_weights():
    fact = math.factorial
    sides = [
        2.0 * (-1.0) ** (k + 1) * fact(6) ** 2 / (k * k * fact(6 - k) * fact(6 + k))
        for k in range(1, 7)
    ]
    return (-2.0 * sum(sides), sides)


CENTER, SIDES = stencil_weights()
KINETIC = -0.5 * (1.0 / 0.36)
SCALE = 2.0 / 11.0
STEP = [SCALE * KINETIC * s for s in SIDES]


def halves(matrix):
    exact = matrix.astype(np.float32)
    high = exact.astype(ml_dtypes.bfloat16)
    low = (exact - high.astype(np.float32)).astype(ml_dtypes.bfloat16)
    return high, low


def band_matrix(size):
    out = np.zeros((size, size))
    for k in range(1, 7):
        for i in range(size - k):
            out[i, i + k] = out[i + k, i] = STEP[k - 1]
    return out


def stencil_operands():
    zh, zl = halves(np.kron(np.eye(4), band_matrix(NZ)))
    xh, xl = halves(band_matrix(NX))
    return np.concatenate([zh, zl], axis=0), np.concatenate([xh, xh, xl], axis=1)


def cost(flops, nbytes):
    return pl.CostEstimate(flops=flops, transcendentals=0, bytes_accessed=nbytes)


def params():
    return pltpu.CompilerParams(vmem_limit_bytes=VMEM)


SMEM_SPEC = pl.BlockSpec(memory_space=pltpu.SMEM)


def masked(states, first, live, p, r):
    slot = lax.broadcasted_iota(jnp.int32, (8, 128), 0) + first
    v = states[p, :, r * 128 : (r + 1) * 128]
    return jnp.where(slot < live, v, 0.0)


def pack_first_body(counts, states0, states1, pot, out):
    band = lax.axis_index("band")
    live = counts[band]
    first = pl.multiple_of(jnp.minimum(band, 6) * (QUAD * 128), 128)
    for p in range(PLANES):
        tiles = [pot[p : p + 1, pl.ds(first + e * 128, 128)] for e in range(QUAD)]
        piece = jnp.concatenate(tiles, axis=0)
        for d in range(16):
            base = (d * PLANES + p) * LINE + TILES
            out[base : base + QUAD, :] = piece

    def plane(p, carry):
        for r in range(TILES):
            for i, states in enumerate((states0, states1)):
                start = 8 * i * PLANES * LINE + p * LINE + r
                out[pl.ds(start, 8, stride=PLANES * LINE), :] = masked(states, 8 * i, live, p, r)
        return carry

    lax.fori_loop(0, PLANES, plane, 0)


def pack_rest_body(counts, states2, states3, states4, out1, out2):
    live = counts[lax.axis_index("band")]

    def plane(p, carry):
        for r in range(TILES):
            for i, states in enumerate((states2, states3)):
                start = 8 * i * ROWS + p * TILES + r
                out1[pl.ds(start, 8, stride=ROWS), :] = masked(states, 16 + 8 * i, live, p, r)
            v = masked(states4, 32, live, p, r)
            for q in range(2):
                out2[pl.ds(8 * q * ROWS + p * TILES + r, 8, stride=ROWS), :] = v
        return carry

    lax.fori_loop(0, PLANES, plane, 0)


def eight(which):
    return pl.BlockSpec((PLANES, 8, CELLS), lambda i: (0, which, 0))


def whole(*shape):
    return pl.BlockSpec(shape, lambda i: (0,) * len(shape))


def pack(counts, states, pot):
    send0 = pl.pallas_call(
        pack_first_body,
        grid=(1,),
        out_shape=jax.ShapeDtypeStruct((NX * LINE, 128), F32),
        in_specs=[SMEM_SPEC, eight(0), eight(1), whole(PLANES, CELLS)],
        out_specs=whole(NX * LINE, 128),
        compiler_params=params(),
        cost_estimate=cost(2_000_000, 4_000_000),
        name="pack0",
    )(counts, states, states, pot)
    send1, send2 = pl.pallas_call(
        pack_rest_body,
        grid=(1,),
        out_shape=(jax.ShapeDtypeStruct((16 * ROWS, 128), F32),) * 2,
        in_specs=[SMEM_SPEC, eight(2), eight(3), eight(4)],
        out_specs=(whole(16 * ROWS, 128),) * 2,
        compiler_params=params(),
        cost_estimate=cost(2_000_000, 6_000_000),
        name="pack1",
    )(counts, states, states, states)
    return send0, send1, send2


def split(value):
    high = value.astype(BF16)
    return high, (value - high.astype(F32)).astype(BF16)


def comp_body(first, half, *refs):
    if first:
        recv = refs[0]
        pots = refs[1:9]
        wz, ax, out, image, diag = refs[9:14]
        refs = refs[14:]
    elif half:
        recv, diag, wz, ax, out, image, part = refs[:7]
        refs = refs[7:]
    else:
        recv, diag, wz, ax, out, image = refs[:6]
        refs = refs[6:]
    va, vb, ua, ub, ha, hb, la, lb, az, ay = refs
    stride = LINE if first else TILES
    zero = jnp.zeros((NX, EDGE), F32)
    for ref in (va, vb, ua, ub):
        ref[:, :EDGE] = zero
        ref[:, EDGE + CELLS :] = zero

    def load(r, carry):
        at = pl.multiple_of(r * 128, 128)
        tiles = [recv[pl.ds(8 * i * stride + r, 8, stride=stride), :] for i in range(12)]
        v = jnp.concatenate(tiles, axis=0)
        va[:, pl.ds(EDGE + at, 128)] = v
        ua[:, pl.ds(EDGE + at, 128)] = pltpu.roll(v, 64, 1)
        high, low = split(v)
        ha[:, pl.ds(at, 128)] = high
        la[:, pl.ds(at, 128)] = low
        return carry

    lax.fori_loop(0, TILES, load, 0)
    if first:
        for s in range(8):
            whose = lax.axis_index("band") ^ s

            @pl.when(whose < 7)
            def _():
                for e in range(QUAD):
                    at = pl.multiple_of(whose * (QUAD * 128) + e * 128, 128)
                    tiles = [
                        pots[s][pl.ds(8 * i * QUAD + e, 8, stride=QUAD), :] for i in range(12)
                    ]
                    diag[:, pl.ds(at, 128)] = (
                        SCALE * (jnp.concatenate(tiles, axis=0) + KINETIC * 3.0 * CENTER) - 2.0
                    )

    low_half = (lax.broadcasted_iota(jnp.int32, (8, GROUP), 1) % 128) < 64

    def apply(src, dst, stage):
        v_src, u_src, h_src, l_src = src
        v_dst, u_dst, h_dst, l_dst = dst

        weights = jnp.concatenate([wz[:256, :], wz[:256, :], wz[256:, :]], axis=0)

        def products(at):
            lefts = []
            for j in range(GROUP // 256):
                h = h_src[:, pl.ds(at + 256 * j, 256)]
                l = l_src[:, pl.ds(at + 256 * j, 256)]
                lefts.append(jnp.concatenate([h, l, h], axis=1))
            along_z = jnp.dot(
                jnp.concatenate(lefts, axis=0), weights, preferred_element_type=F32
            )
            h = h_src[:, pl.ds(at, GROUP)]
            l = l_src[:, pl.ds(at, GROUP)]
            along_x = jnp.dot(
                ax[...], jnp.concatenate([h, l, h], axis=0), preferred_element_type=F32
            )
            return along_z, along_x

        az[...], ay[...] = products(0)

        def block(group, carry):
            at = pl.multiple_of(group * GROUP, GROUP)
            after = jnp.minimum(group + 1, CELLS // GROUP - 1)
            next_z, next_x = products(pl.multiple_of(after * GROUP, GROUP))
            pending = []
            for i in range(12):
                rows = slice(8 * i, 8 * i + 8)
                v = v_src[rows, pl.ds(at, GROUP + 2 * EDGE)]
                u = u_src[rows, pl.ds(at, GROUP + 2 * EDGE)]

                def v_at(k):
                    return v[:, EDGE + 128 * k : EDGE + 128 * k + GROUP]

                def u_at(k):
                    return u[:, EDGE + 128 * k : EDGE + 128 * k + GROUP + 128]

                odd = STEP[0] * (u_at(0) + u_at(-1))
                odd = odd + STEP[2] * (u_at(1) + u_at(-2))
                odd = odd + STEP[4] * (u_at(2) + u_at(-3))
                even = STEP[1] * (v_at(1) + v_at(-1))
                even = even + STEP[3] * (v_at(2) + v_at(-2))
                even = even + STEP[5] * (v_at(3) + v_at(-3))
                near = even + jnp.where(low_half, odd[:, :GROUP], odd[:, 128:])
                center = v_at(0)
                new = near + diag[rows, pl.ds(at, GROUP)] * center
                new = new + ay[rows, :]
                across = [slice(NX * j + 8 * i, NX * j + 8 * i + 8) for j in range(GROUP // 256)]
                new = new + jnp.concatenate([az[strip, :] for strip in across], axis=1)
                ay[rows, :] = next_x[rows, :]
                for strip in across:
                    az[strip, :] = next_z[strip, :]
                if stage == 1:
                    new = 0.5 * new
                elif stage < 4:
                    new = new - v_dst[rows, pl.ds(EDGE + at, GROUP)]
                else:
                    new = 5.5 * new + 11.0 * center
                v_dst[rows, pl.ds(EDGE + at, GROUP)] = new
                if stage < 4:
                    for j in range(GROUP // 128):
                        u_dst[rows, pl.ds(EDGE + at + 128 * j, 128)] = pltpu.roll(
                            new[:, 128 * j : 128 * j + 128], 64, 1
                        )
                    pending.append(new)
                    if i % 2:
                        high, low = split(jnp.concatenate(pending, axis=0))
                        pair = slice(8 * i - 8, 8 * i + 8)
                        h_dst[pair, pl.ds(at, GROUP)] = high
                        l_dst[pair, pl.ds(at, GROUP)] = low
                        pending = []
            return carry

        lax.fori_loop(0, CELLS // GROUP, block, 0, unroll=True if half or first else 1)

    a, b = (va, ua, ha, la), (vb, ub, hb, lb)
    apply(a, b, 1)
    apply(b, a, 2)
    apply(a, b, 3)
    apply(b, a, 4)
    outs = [(out, 1, 0), (image, 0, 0)]
    if half:
        outs.append((part, 1, (lax.axis_index("dom") // 8) * (12 * 128)))

    for ref, which, begin in outs:
        count = ref.shape[0] // NX

        def store(r, carry):
            at = pl.multiple_of(EDGE + begin + r * 128, 128)
            for i in range(12):
                ref[pl.ds(8 * i * count + r, 8, stride=count), :] = (vb if which else va)[
                    8 * i : 8 * i + 8, pl.ds(at, 128)
                ]
            return carry

        lax.fori_loop(0, count, store, 0)


def comp(first, half, args):
    out_shape = [jax.ShapeDtypeStruct((NX * TILES, 128), F32)] * 2
    if first:
        out_shape.append(jax.ShapeDtypeStruct((NX, CELLS), F32))
    if half:
        out_shape.append(jax.ShapeDtypeStruct((NX * HALF, 128), F32))
    wide = pltpu.VMEM((NX, WIDE), F32)
    narrow = pltpu.VMEM((NX, CELLS), BF16)
    in_specs = [pl.BlockSpec()] * len(args)

    def body(*refs):
        comp_body(first, half, *refs)

    return pl.pallas_call(
        body,
        out_shape=tuple(out_shape),
        in_specs=in_specs,
        scratch_shapes=[wide] * 4
        + [narrow] * 4
        + [pltpu.VMEM((NX * GROUP // 256, 256), F32), pltpu.VMEM((NX, GROUP), F32)],
        compiler_params=params(),
        cost_estimate=cost(15_000_000_000, 10_000_000),
    )(*args)


def unpack_body(*refs):
    recv, sends, send = refs[0], refs[-9:-1], refs[-1]
    filtered = refs[-10]
    band = lax.axis_index("band")
    for p in range(PLANES):
        for r in range(TILES):
            b, t = divmod(p * TILES + r, PARTS)
            for i in range(2):
                v = recv[pl.ds(8 * i * ROWS + p * TILES + r, 8, stride=ROWS), :]
                rows = slice(8 * i, 8 * i + 8)
                send[b ^ band, rows, t * 128 : (t + 1) * 128] = v
                filtered[p, rows, r * 128 : (r + 1) * 128] = v
    for s in range(8):
        sends[s][...] = send[s]


def unpack(which, recv, base):
    count = 16

    def body(*refs):
        unpack_body(*refs)

    in_specs, args = [whole(*recv.shape)], (recv,)
    if which:
        in_specs.append(pl.BlockSpec(memory_space=pl.ANY))
        args += (base,)
    return pl.pallas_call(
        body,
        grid=(1,),
        out_shape=(jax.ShapeDtypeStruct((PLANES, CAP, CELLS), F32),)
        + (jax.ShapeDtypeStruct((count, WIDTH), F32),) * 8,
        in_specs=in_specs,
        out_specs=(
            pl.BlockSpec((PLANES, count, CELLS), lambda i: (0, which, 0)),
        )
        + (whole(count, WIDTH),) * 8,
        scratch_shapes=[pltpu.VMEM((8, count, WIDTH), F32)],
        input_output_aliases={1: 0} if which else {},
        compiler_params=params(),
        cost_estimate=cost(4_000_000, 4_000_000),
    )(*args)


def unpack_rest_body(recv, base, filtered):
    for p in range(PLANES):
        for r in range(TILES):
            q = r // HALF
            start = 8 * q * PLANES * HALF + p * HALF + r - 12 * q
            filtered[p, :, r * 128 : (r + 1) * 128] = recv[
                pl.ds(start, 8, stride=PLANES * HALF), :
            ]


def unpack_rest(recv, base):
    return pl.pallas_call(
        unpack_rest_body,
        grid=(1,),
        out_shape=jax.ShapeDtypeStruct((PLANES, CAP, CELLS), F32),
        in_specs=[
            pl.BlockSpec((16 * PLANES * HALF, 128), lambda i: (0, 0)),
            pl.BlockSpec(memory_space=pl.ANY),
        ],
        out_specs=pl.BlockSpec((PLANES, 8, CELLS), lambda i: (0, 4, 0)),
        input_output_aliases={1: 0},
        compiler_params=params(),
        cost_estimate=cost(1_000_000, 2_000_000),
        name="unpack_rest",
    )(recv, base)


def share_body(img0, img1, img2, f2, out):
    second = lax.axis_index("dom") >= 8

    def group(big, carry):
        base = pl.multiple_of(big * 8 * PARTS, 8)
        to = pl.multiple_of(big * 8 * 64, 8)
        for g in range(8):
            at = base + PARTS * g
            row = to + 64 * g
            out[pl.ds(row, PARTS), :] = img0[pl.ds(at, PARTS), :]
            out[pl.ds(row + PARTS, PARTS), :] = img1[pl.ds(at, PARTS), :]
            for ref, start in ((img2, 2 * PARTS), (f2, 2 * PARTS + SHARE)):
                out[pl.ds(row + start, SHARE), :] = jnp.where(
                    second, ref[pl.ds(at + 10, SHARE), :], ref[pl.ds(at, SHARE), :]
                )
        return carry

    lax.fori_loop(0, 16, group, 0)


def share(img0, img1, img2, f2):
    return pl.pallas_call(
        share_body,
        out_shape=jax.ShapeDtypeStruct((128 * 64, 128), F32),
        compiler_params=params(),
        cost_estimate=cost(2_000_000, 10_000_000),
        name="share",
    )(img0, img1, img2, f2)


SLOTS = 8 * CAP
SECOND = 384
BOTH = SECOND + SLOTS
KSTEP = 7 * 128


def gram_body(*refs):
    band = lax.axis_index("band")
    pieces, (rest, out, main, high, low, total) = refs[:16], refs[16:]
    for s in range(8):
        for k in range(2):
            main[band ^ s, 16 * k : 16 * k + 16] = pieces[8 * k + s][...]
    high[SLOTS:SECOND, :] = jnp.zeros((SECOND - SLOTS, PARTS * 128), BF16)
    low[SLOTS:SECOND, :] = jnp.zeros((SECOND - SLOTS, PARTS * 128), BF16)

    def fill(t, carry, late):
        at = pl.multiple_of(t * 128, 128)
        f_rows = []
        i_rows = []
        for b in range(8):
            shared = [
                rest[
                    pl.ds((8 * late * 8 + b) * 64 + start + t - 10 * late, 8, stride=8 * 64), :
                ]
                for start in (2 * PARTS, 2 * PARTS + SHARE)
            ]
            f_rows += [main[b, :, pl.ds(at, 128)], shared[1]]
            for k in range(2):
                for half in range(2):
                    start = (64 * half + b) * 64 + PARTS * k + t
                    i_rows.append(rest[pl.ds(start, 8, stride=8 * 64), :])
            i_rows.append(shared[0])
        for rows, base in ((f_rows, 0), (i_rows, SECOND)):
            h, l = split(jnp.concatenate(rows, axis=0))
            high[base : base + SLOTS, pl.ds(at, 128)] = h
            low[base : base + SLOTS, pl.ds(at, 128)] = l
        return carry

    lax.fori_loop(0, SHARE, lambda t, c: fill(t, c, 0), 0)
    lax.fori_loop(SHARE, PARTS, lambda t, c: fill(t, c, 1), 0)
    total[...] = jnp.zeros(total.shape, F32)

    def step(k, carry):
        cols = pl.ds(pl.multiple_of(k * KSTEP, 128), KSTEP)
        term = None
        for one, two in ((high, high), (high, low), (low, high)):
            part = lax.dot_general(
                one[:SLOTS, cols],
                two[:, cols],
                (((1,), (1,)), ((), ())),
                preferred_element_type=F32,
            )
            term = part if term is None else term + part
        total[...] += term
        return carry

    lax.fori_loop(0, PARTS * 128 // KSTEP, step, 0)
    for d in range(16):
        out[d, :20, :] = total[20 * d : 20 * d + 20, :SLOTS]
        out[d, 20:40, :] = total[20 * d : 20 * d + 20, SECOND:]


def gram(pieces, rest):
    return pl.pallas_call(
        gram_body,
        out_shape=jax.ShapeDtypeStruct((16, 40, SLOTS), F32),
        scratch_shapes=[pltpu.VMEM((8, MAIN, PARTS * 128), F32)]
        + [pltpu.VMEM((BOTH, PARTS * 128), BF16)] * 2
        + [pltpu.VMEM((SLOTS, BOTH), F32)],
        compiler_params=params(),
        cost_estimate=cost(4_000_000_000, 8_000_000),
        name="gram",
    )(*pieces, rest)


def exchange(value, axis, parts):
    shape = value.shape
    value = value.reshape((parts, -1) + shape[-1:])
    return lax.all_to_all(value, axis, 0, 0, tiled=True).reshape(shape)


def swaps(pieces):
    out = [pieces[0]]
    for s in range(1, 8):
        pairs = [(b, b ^ s) for b in range(8)]
        out.append(lax.ppermute(pieces[s], "band", pairs))
    return out


def work(states, potential, counts):
    wz, ax = (jnp.asarray(m) for m in stencil_operands())
    send0, send1, send2 = pack(counts, jnp.transpose(states, (1, 0, 2)), potential)
    recv0 = exchange(send0, "dom", 16)
    own = recv0.reshape(NX, LINE, 128)[:, TILES:, :].reshape(NX * QUAD, 128)
    pots = swaps([own] * 8)
    recv1 = exchange(send1, "dom", 16)
    out0, img0, diag = comp(True, False, (recv0, *pots, wz, ax))
    recv2 = exchange(send2, "dom", 16)
    out1, img1 = comp(False, False, (recv1, diag, wz, ax))
    back0 = exchange(out0, "dom", 16)
    filtered, *early = unpack(0, back0, None)
    early = swaps(early)
    recv2, filtered = lax.optimization_barrier((recv2, filtered))
    out2, img2, half2 = comp(False, True, (recv2, diag, wz, ax))
    back1 = exchange(out1, "dom", 16)
    back2 = exchange(half2, "dom", 16)
    filtered, *late = unpack(1, back1, filtered)
    late = swaps(late)
    img0, filtered = lax.optimization_barrier((img0, filtered))
    shared = share(img0, img1, img2, out2)
    rest = exchange(shared, ("dom", "band"), 128)
    filtered = unpack_rest(back2, filtered)
    terms = gram(early + late, rest)
    terms = lax.all_to_all(terms, "dom", 0, 0, tiled=True).sum(axis=0)
    terms = jnp.transpose(terms.reshape(2, 20, 8, CAP), (2, 0, 1, 3)).reshape(8, 40, CAP)
    terms = lax.all_to_all(terms, "band", 0, 0, tiled=True).sum(axis=0)
    projected = jnp.transpose(terms.reshape(2, 20, CAP), (0, 2, 1))
    return (jnp.transpose(filtered, (1, 0, 2)), projected)


def solution(mesh):
    return jax.shard_map(
        work,
        mesh=mesh,
        in_specs=(P("band", "dom", None), P("dom", None), P()),
        out_specs=(P("band", "dom", None), P(None, "band", "dom")),
        check_vma=False,
    )
```
